256 devices in a mesh: ia: 16 (over x, z_lo), jb: 16 (over z_hi, y, core).
Axes of the slice: x: 4, y: 4, z: 8 (z_hi: 2, z_lo: 4; z = z_hi * 4 + z_lo), core: 2. Of those that a mesh axis runs over, the one named last changes fastest.
Arguments:
- cycle_w: bfloat16 [16384, 16384], P('ia', 'jb'), may hold values from -0.046875 to 0.046875
- amplitudes: bfloat16 [16384, 4096], P('jb', 'ia'), may hold values from -6 to 6
- fock_vir: float32 [512, 512], replicated, may hold values from -0.25 to 0.25
- energy_i: float32 [32], replicated, may hold values from -2 to -0.5
- energy_j: float32 [8], replicated, may hold values from -2 to -0.5
- energy_vir: float32 [512], replicated, may hold values from 0.3 to 3
Outputs:
- new_amplitudes: float32 [16384, 4096], P('ia', 'jb')
The draws below stay inside these ranges and needn't reach their ends.
All inputs are finite; a program needn't handle non-finite values.
Results may differ from the reference program's by a relative error of at most 0.0003.
Values may be sent and summed in bfloat16 or wider, within the bound.
A program may use at most 128 MiB of HBM per device.

```python
import jax
import jax.numpy as jnp
from jax import lax

V = 512
KO = 32
OCC_I = 32
OCC_J = 8


def with_spikes(entries, rng, source, target, parts, factor):
    owner, partner = [(jnp.arange(entries.shape[axis_at]) // (entries.shape[axis_at] // parts)).reshape([-1 if axis == axis_at else 1 for axis in range(entries.ndim)]) for axis_at in (source, target)]
    chosen = jax.random.permutation(rng, parts)[partner]
    strong = (owner == chosen) | (owner == (partner + parts // 2) % parts)
    return jnp.where(strong, factor * entries, entries)


def shard_levels(rng, extent, shards, low, top_value):
    level = 1.0
    for position, shards_of in shards:
        steps = jax.random.uniform(jax.random.fold_in(jax.random.fold_in(rng, 6), position), (shards_of,), jnp.float32, low / len(shards), top_value / len(shards))
        level = level * jnp.repeat(jnp.exp(steps), extent[position] // shards_of).reshape((-1,) + (1,) * (len(extent) - 1 - position))
    return level


def normal_values(key, extent, width, most, split=(), dtype=jnp.bfloat16):
    entries = width * jax.random.normal(key, extent, jnp.float32)
    if split:
        entries = entries * shard_levels(key, extent, split, -0.22, 0.18)
    return jnp.clip(entries, -most, most).astype(dtype)


def bell_draw_with(own_key, extent, deviation, bound, cuts, heavy, kind=jnp.bfloat16):
    result = deviation * jax.random.normal(own_key, extent, jnp.float32)
    if cuts:
        result = result * shard_levels(own_key, extent, cuts, -0.22, 0.18)
    return jnp.clip(with_spikes(result, jax.random.fold_in(own_key, 3), *heavy), -bound, bound).astype(kind)


def setup_inputs(seed: int = 0) -> dict:
    streams_of = jax.random.split(jax.random.key(seed), 7)
    return {
        "cycle_w": normal_values(streams_of[0], (OCC_I * V, KO * V), (KO * V) ** -0.5, 0.046875, ((0, 16), (1, 16))),
        "amplitudes": bell_draw_with(streams_of[1], (KO * V, OCC_J * V), 1.0, 6.0, ((0, 16), (1, 16)), (0, 1, 16, 2.0)),
        "fock_vir": normal_values(streams_of[2], (V, V), V ** -0.5, 0.25, (), jnp.float32),
        "energy_i": jnp.clip(jax.random.uniform(streams_of[3], (OCC_I,), jnp.float32, -2.0, -0.5), -2.0, -0.5),
        "energy_j": jnp.clip(jax.random.uniform(streams_of[4], (OCC_J,), jnp.float32, -2.0, -0.5), -2.0, -0.5),
        "energy_vir": jnp.clip(jax.random.uniform(streams_of[5], (V,), jnp.float32, 0.3, 3.0), 0.3, 3.0),
    }


def reference(cycle_w, amplitudes, fock_vir, energy_i, energy_j, energy_vir):
    cycle = jnp.dot(cycle_w, amplitudes, preferred_element_type=jnp.float32)
    blocks = cycle.reshape(OCC_I, V, OCC_J, V)
    left = jnp.einsum('ac,icjb->iajb', fock_vir, blocks, precision=lax.Precision.HIGHEST)
    right = jnp.einsum('iajd,bd->iajb', blocks, fock_vir, precision=lax.Precision.HIGHEST)
    dressed = blocks + left + right
    denom = energy_i[:, None, None, None] + energy_j[None, None, :, None] - energy_vir[None, :, None, None] - energy_vir[None, None, None, :]
    return (dressed / denom).reshape(OCC_I * V, OCC_J * V)
```

```python
import functools

import jax
import jax.numpy as jnp
from jax import lax
from jax.experimental import pallas as pl
from jax.experimental.pallas import tpu as pltpu
from jax.sharding import PartitionSpec as P

F32 = jnp.float32
BF16 = jnp.bfloat16
MESH = pl.DeviceIdType.MESH

UNITS = (
    ((0, 0, 0), (0, 0, 1)),
    ((-1, 0, 0), (1, 0, 1)),
    ((0, 1, 0), (0, 1, 1)),
    ((-1, 0, 1), (1, 0, 0)),
    ((2, 0, 0), (2, 0, 1)),
    ((-1, 1, 0), (1, 1, 1)),
    ((-1, 1, 1), (1, 1, 0)),
    ((2, 1, 0), (2, 1, 1)),
)
EVENTS = len(UNITS)


def div(a, b):
    return lax.div(a, jnp.int32(b))


def rem(a, b):
    return lax.rem(a, jnp.int32(b))


def split(value):
    high = value.astype(BF16)
    return high, (value - high.astype(F32)).astype(BF16)


def dot3(a, b, dims):
    dot = functools.partial(
        lax.dot_general, dimension_numbers=(dims, ((), ())), preferred_element_type=F32
    )
    return dot(a[0], b[0]) + (dot(a[0], b[1]) + dot(a[1], b[0]))


def kernel(
    w_hbm, a_hbm, fock_hbm, ei_ref, ej_ref, ev_ref, out_ref,
    w2, a2, cb, full, half, relay, rz, racc, roth, rec, fock, fhi, flo,
    loc, wx, ax, recv_a, send_x, send_z, r_half, r_full, send_y,
    r_relay, send_r, send_f, r_final, cx,
):
    M, K = w_hbm.shape
    NB = a_hbm.shape[1]
    HB = NB // 2
    V = fock_hbm.shape[0]
    HM = M // 2

    ia = lax.axis_index("ia")
    jb = lax.axis_index("jb")
    x, zl = div(ia, 4), rem(ia, 4)
    zh, y, c = div(jb, 8), rem(div(jb, 2), 4), rem(jb, 2)
    z = zh * 4 + zl
    f = div(zl, 2)
    g = 1 - f
    owner = c == rem(zl, 2)

    def dev(x=x, y=y, z=z, c=c):
        return {"ia": x * 4 + rem(z, 4), "jb": div(z, 4) * 8 + y * 2 + c}

    xp, xm = dev(x=rem(x + 1, 4)), dev(x=rem(x + 3, 4))
    yp, ym = dev(y=rem(y + 1, 4)), dev(y=rem(y + 3, 4))
    zp2, zm2 = dev(z=rem(z + 2, 8)), dev(z=rem(z + 6, 8))
    up, down = dev(z=rem(z + 1, 8)), dev(z=rem(z + 7, 8))
    partner = dev(c=1 - c)
    has_up, has_down = zl < 3, zl > 0

    def remote(src, dst, send, recv, to):
        return pltpu.make_async_remote_copy(
            src_ref=src, dst_ref=dst, send_sem=send, recv_sem=recv,
            device_id=to, device_id_type=MESH,
        )

    krows = pl.ds(pl.multiple_of(c * K, K), K)
    w_local = pltpu.make_async_copy(w_hbm, w2.at[:, krows], loc.at[0])
    a_local = pltpu.make_async_copy(a_hbm, a2.at[0, krows, :], loc.at[1])
    f_local = pltpu.make_async_copy(fock_hbm, fock, loc.at[2])

    @pl.when(owner)
    def _():
        a_local.start()

    w_local.start()
    f_local.start()

    barrier = pltpu.get_barrier_semaphore()
    for to in (partner, xp, xm, yp, ym, zp2, zm2):
        pl.semaphore_signal(barrier, inc=1, device_id=to, device_id_type=MESH)

    @pl.when(has_up)
    def _():
        pl.semaphore_signal(barrier, inc=1, device_id=up, device_id_type=MESH)

    @pl.when(has_down)
    def _():
        pl.semaphore_signal(barrier, inc=1, device_id=down, device_id_type=MESH)

    pl.semaphore_wait(barrier, 7 + has_up.astype(jnp.int32) + has_down.astype(jnp.int32))

    a_swap = remote(a_hbm, a2.at[0, krows, :], ax.at[0], ax.at[1], partner)
    w_swap = remote(w_hbm, w2.at[:, krows], wx.at[0], wx.at[1], partner)

    @pl.when(jnp.logical_not(owner))
    def _():
        a_swap.start()

    w_swap.start()

    def a_unit(ev, j):
        return a2.at[ev, :, pl.ds(j * HB, HB)]

    def a_wait(ev, j):
        remote(a_unit(ev, j), a_unit(ev, j), send_x.at[0, 0], recv_a.at[ev, j], xp).wait_recv()

    def a_send_x(direction, index, src, ev, j):
        return remote(
            src, a_unit(ev, j), send_x.at[direction, index], recv_a.at[ev, j],
            xp if direction == 0 else xm,
        )

    def a_sends_of(blk):
        ev = 2 * blk
        s = f if blk == 0 else g
        origin = 2 * s + c
        zs, xs = [], []
        for h in range(2):
            there = div(zl + 1, 2)
            ev_up = jnp.where(s == there, 0, 2)
            zs.append((
                jnp.logical_and(has_up, zl >= origin),
                remote(a_unit(ev, h), a_unit(ev_up, h), send_z.at[blk, 0, h], recv_a.at[ev_up, h], up),
            ))
            below = div(zl + 1, 2) - 1
            ev_down = jnp.where(s == below, 0, 2)
            zs.append((
                jnp.logical_and(has_down, zl <= origin),
                remote(a_unit(ev, h), a_unit(ev_down, h), send_z.at[blk, 1, h], recv_a.at[ev_down, h], down),
            ))
        near, far = (1, 3) if blk == 0 else (5, 6)
        for direction in range(2):
            for h in range(2):
                order = h if direction == 0 else 1 - h
                xs.append(a_send_x(
                    direction, 3 * blk + order, a_unit(ev, h), near if order == 0 else far, direction,
                ))
        return zs, xs

    def a_forwards(blk):
        ev, to = (1, 4) if blk == 0 else (5, 7)
        return [a_send_x(d, 3 * blk + 2, a_unit(ev, d), to, d) for d in range(2)]

    def get_a(ev):
        if ev in (0, 2):
            zs, xs = a_sends_of(ev // 2)
            if ev == 0:
                @pl.when(owner)
                def _():
                    a_local.wait()
                    remote(a_hbm, a2.at[0, pl.ds(pl.multiple_of((1 - c) * K, K), K), :], ax.at[0], ax.at[1], partner).wait_recv()
            for h in range(2):
                if ev == 0:
                    @pl.when(jnp.logical_not(owner))
                    def _():
                        a_wait(0, h)
                else:
                    a_wait(ev, h)
                for cond, copy in zs[2 * h:2 * h + 2]:
                    @pl.when(cond)
                    def _():
                        copy.start()
                xs[h].start()
            xs[3].start()
            xs[2].start()
            return
        forwards = a_forwards(0) if ev == 1 else a_forwards(1) if ev == 5 else None
        for j in range(2):
            a_wait(ev, j)
            if forwards:
                forwards[j].start()

    def compute(ev):
        def rows(i, _):
            at = pl.ds(pl.multiple_of(i * HM, HM), HM)
            cb[ev, at, :] = jnp.dot(w2[at, :], a2[ev], preferred_element_type=F32)
            return 0

        lax.fori_loop(0, 2, rows, 0)

    def c_part(ev, j, part):
        return cb.at[ev, pl.ds(part * HM, HM), pl.ds(j * HB, HB)]

    def c_send(ev, j, part, dst, recv, to):
        return remote(c_part(ev, j, part), dst, send_y.at[ev, j, part], recv, to)

    def place(ev, j):
        rel, far, h = UNITS[ev][j]
        xb = rem(x + (rel + 4), 4)
        s = g if far else f
        zd = div(xb, 2)
        yd = 2 * rem(xb, 2) + s
        return zd, rem(yd - y + 4, 4), h

    def to_half(ev, j, part, zd, h):
        slot = zd * 4 + part * 2 + h
        return c_send(ev, j, part, half.at[slot], r_half.at[slot], yp if part == 0 else ym)

    def to_full(ev, j, part, zd, h, side):
        slot = zd * 4 + side * 2 + h
        return c_send(
            ev, j, part, full.at[slot, pl.ds(part * HM, HM), :], r_full.at[slot, part],
            yp if side == 0 else ym,
        )

    def y_first(ev):
        for j in range(2):
            zd, r, h = place(ev, j)

            @pl.when(r == 2)
            def _():
                to_half(ev, j, 0, zd, h).start()
                to_half(ev, j, 1, zd, h).start()

            @pl.when(r == 1)
            def _():
                to_full(ev, j, 1, zd, h, 0).start()

            @pl.when(r == 3)
            def _():
                to_full(ev, j, 0, zd, h, 1).start()

    def y_second(ev):
        for j in range(2):
            zd, r, h = place(ev, j)
            for side, part in ((0, 0), (1, 1)):
                @pl.when(r == 1 + 2 * side)
                def _():
                    to_half(ev, j, part, zd, h).wait_recv()
                    slot = zd * 4 + part * 2 + h
                    at = (ev, pl.ds(part * HM, HM), pl.ds(j * HB, HB))
                    cb[at] = cb[at] + half[slot]
                    to_full(ev, j, part, zd, h, side).start()

    def to_relay(ev, j, part, h):
        return remote(
            c_part(ev, j, part), relay.at[part * 2 + h], send_r.at[part * 2 + h],
            r_relay.at[part * 2 + h], zp2 if part == 0 else zm2,
        )

    def y_last(ev):
        for j in range(2):
            zd, r, h = place(ev, j)

            @pl.when(r == 0)
            def _():
                for side in range(2):
                    for part in range(2):
                        to_full(ev, j, part, zd, h, side).wait_recv()
                cols = pl.ds(j * HB, HB)
                total = cb[ev, :, cols] + full[zd * 4 + h] + full[zd * 4 + 2 + h]

                @pl.when(zd == zh)
                def _():
                    racc[:, pl.ds(h * HB, HB)] = total

                @pl.when(zd != zh)
                def _():
                    cb[ev, :, cols] = total
                    to_relay(ev, j, 0, h).start()
                    to_relay(ev, j, 1, h).start()

    def to_final(part, h):
        return remote(
            relay.at[part * 2 + h], rz.at[h, pl.ds(part * HM, HM), :], send_f.at[part * 2 + h],
            r_final.at[part * 2 + h], zp2 if part == 0 else zm2,
        )

    def event_of(source, h):
        xb = 2 * (1 - div(source, 4)) + div(y, 2)
        rel = rem(xb - x + 4, 4)
        isf = rem(y, 2) == div(rem(source, 4), 2)
        near, far = jnp.where(isf, 1, 5), jnp.where(isf, 3, 6)
        side = (near, far) if h == 0 else (far, near)
        own, opposite = jnp.where(isf, 0, 2), jnp.where(isf, 4, 7)
        return jnp.where(
            rel == 0, own, jnp.where(rel == 2, opposite, jnp.where(rel == 3, side[0], side[1]))
        )

    def z_relay(step):
        for part in range(2):
            source = rem(z + (6 if part == 0 else 2), 8)
            for h in range(2):
                @pl.when(event_of(source, h) == step)
                def _():
                    remote(
                        relay.at[part * 2 + h], relay.at[part * 2 + h], send_r.at[part * 2 + h],
                        r_relay.at[part * 2 + h], zp2,
                    ).wait_recv()
                    to_final(part, h).start()

    def prepare():
        f_local.wait()
        fhi[...], flo[...] = split(fock[...])
        levels = jnp.broadcast_to(ev_ref[...], (128, V)).T
        here = ev_ref[:, pl.ds(pl.multiple_of(c * NB, NB), NB)]
        for i in range(M // V):
            pair = ei_ref[ia * (M // V) + i] + ej_ref[div(jb, 2)]
            for k in range(NB // 128):
                cols = pl.ds(k * 128, 128)
                denom = pair - levels - here[:, k * 128:(k + 1) * 128]
                rec[pl.ds(i * V, V), cols] = 1.0 / denom

    for step in range(EVENTS + 4):
        if step < EVENTS:
            get_a(step)
            if step == 0:
                w_local.wait()
                remote(w_hbm, w2.at[:, pl.ds(pl.multiple_of((1 - c) * K, K), K)], wx.at[0], wx.at[1], partner).wait_recv()
            compute(step)
            y_first(step)
            if step == 0:
                prepare()
        if 0 <= step - 1 < EVENTS:
            y_second(step - 1)
        if 0 <= step - 2 < EVENTS:
            y_last(step - 2)
        if 0 <= step - 3 < EVENTS:
            z_relay(step - 3)

    for h in range(2):
        for part in range(2):
            to_final(part, h).wait_recv()
        cols = pl.ds(h * HB, HB)
        racc[:, cols] = racc[:, cols] + rz[h]

    swap = remote(racc, roth, cx.at[0], cx.at[1], partner)
    swap.start()

    mine = pl.ds(pl.multiple_of(c * NB, NB), NB)
    other = pl.ds(pl.multiple_of((1 - c) * NB, NB), NB)
    nn, nt = ((1,), (0,)), ((1,), (1,))
    for i in range(M // V):
        at = pl.ds(i * V, V)
        value = racc[at, :]
        parts = split(value)
        rows = value + dot3((fhi[...], flo[...]), parts, nn)
        out_ref[at, :] = rows + dot3(parts, (fhi[mine, mine], flo[mine, mine]), nt)
    swap.wait_recv()
    for i in range(M // V):
        at = pl.ds(i * V, V)
        parts = split(roth[at, :])
        out_ref[at, :] = (
            out_ref[at, :] + dot3(parts, (fhi[mine, other], flo[mine, other]), nt)
        ) * rec[at, :]

    swap.wait_send()
    w_swap.wait_send()

    @pl.when(jnp.logical_not(owner))
    def _():
        a_swap.wait_send()

    for blk in range(2):
        zs, xs = a_sends_of(blk)
        for cond, copy in zs:
            @pl.when(cond)
            def _():
                copy.wait_send()
        for copy in xs + a_forwards(blk):
            copy.wait_send()
    for ev in range(EVENTS):
        for j in range(2):
            zd, r, h = place(ev, j)

            @pl.when(r != 0)
            def _():
                for part in range(2):
                    to_half(ev, j, part, zd, h).wait_send()
    for part in range(2):
        for h in range(2):
            to_relay(0, 0, part, h).wait_send()
            to_final(part, h).wait_send()


def per_device(cycle_w, amplitudes, fock_vir, energy_i, energy_j, energy_vir):
    M, K = cycle_w.shape
    NB = amplitudes.shape[1]
    HB, HM = NB // 2, M // 2
    V = fock_vir.shape[0]
    dma = pltpu.SemaphoreType.DMA
    anywhere = pl.BlockSpec(memory_space=pl.ANY)
    vmem = pl.BlockSpec(memory_space=pltpu.VMEM)
    smem = pl.BlockSpec(memory_space=pltpu.SMEM)
    return pl.pallas_call(
        kernel,
        out_shape=jax.ShapeDtypeStruct((M, NB), F32),
        in_specs=[anywhere, anywhere, anywhere, smem, smem, vmem],
        out_specs=vmem,
        scratch_shapes=[
            pltpu.VMEM((M, 2 * K), BF16),
            pltpu.VMEM((EVENTS, 2 * K, NB), BF16),
            pltpu.VMEM((EVENTS, M, NB), F32),
            pltpu.VMEM((8, M, HB), F32),
            pltpu.VMEM((8, HM, HB), F32),
            pltpu.VMEM((4, HM, HB), F32),
            pltpu.VMEM((2, M, HB), F32),
            pltpu.VMEM((M, NB), F32),
            pltpu.VMEM((M, NB), F32),
            pltpu.VMEM((M, NB), F32),
            pltpu.VMEM((V, V), F32),
            pltpu.VMEM((V, V), BF16),
            pltpu.VMEM((V, V), BF16),
            dma((3,)), dma((2,)), dma((2,)), dma((EVENTS, 2)), dma((2, 6)), dma((2, 2, 2)),
            dma((8,)), dma((8, 2)), dma((EVENTS, 2, 2)),
            dma((4,)), dma((4,)), dma((4,)), dma((4,)), dma((2,)),
        ],
        compiler_params=pltpu.CompilerParams(
            collective_id=0, has_side_effects=True, vmem_limit_bytes=60 * 1024 * 1024
        ),
        name="residual",
    )(cycle_w, amplitudes, fock_vir, energy_i, energy_j, energy_vir.reshape(1, -1))


def solution(mesh):
    in_specs = (P("ia", "jb"), P("jb", "ia"), P(), P(), P(), P())
    out_specs = P("ia", "jb")
    return jax.shard_map(
        per_device, mesh=mesh, in_specs=in_specs, out_specs=out_specs, check_vma=False
    )
```

```python
import functools

import jax
import jax.numpy as jnp
from jax import lax
from jax.experimental import pallas as pl
from jax.experimental.pallas import tpu as pltpu
from jax.sharding import PartitionSpec as P

F32 = jnp.float32
BF16 = jnp.bfloat16
MESH = pl.DeviceIdType.MESH

UNITS = (
    ((0, 0, 0), (0, 0, 1)),
    ((-1, 0, 0), (1, 0, 1)),
    ((-1, 0, 1), (1, 0, 0)),
    ((0, 1, 0), (0, 1, 1)),
    ((-1, 1, 0), (1, 1, 1)),
    ((2, 0, 0), (2, 0, 1)),
    ((-1, 1, 1), (1, 1, 0)),
    ((2, 1, 0), (2, 1, 1)),
)
OWN, NEAR, FAR, OPPOSITE = (0, 3), (1, 4), (2, 6), (5, 7)
EVENTS = len(UNITS)

LEVEL = 10
BASE = 2 * LEVEL + 1
REST = 2.0 ** -8 / LEVEL
TINY = 1e-30
CHUNK = 64


def div(a, b):
    return lax.div(a, jnp.int32(b))


def rem(a, b):
    return lax.rem(a, jnp.int32(b))


def split(value):
    high = value.astype(BF16)
    return high, (value - high.astype(F32)).astype(BF16)


def dot3(a, b, dims):
    dot = functools.partial(
        lax.dot_general, dimension_numbers=(dims, ((), ())), preferred_element_type=F32
    )
    return dot(a[0], b[0]) + (dot(a[0], b[1]) + dot(a[1], b[0]))


def kernel(
    w_hbm, a_hbm, fock_hbm, ei_ref, ej_ref, ev_ref, out_ref,
    w2, a2, cb, sent, full, half, rz, racc, roth, rec, fock, fhi, flo,
    loc, wx, ax, recv_a, send_x, send_z, r_half, r_full, send_y,
    send_f, r_final, cx,
):
    M, K = w_hbm.shape
    NB = a_hbm.shape[1]
    HB = NB // 2
    V = fock_hbm.shape[0]
    HM = M // 2

    ia = lax.axis_index("ia")
    jb = lax.axis_index("jb")
    x, zl = div(ia, 4), rem(ia, 4)
    zh, y, c = div(jb, 8), rem(div(jb, 2), 4), rem(jb, 2)
    z = zh * 4 + zl
    f = div(zl, 2)
    g = 1 - f
    owner = c == rem(zl, 2)

    def dev(x=x, y=y, z=z, c=c):
        return {"ia": x * 4 + rem(z, 4), "jb": div(z, 4) * 8 + y * 2 + c}

    xp, xm = dev(x=rem(x + 1, 4)), dev(x=rem(x + 3, 4))
    yp, ym = dev(y=rem(y + 1, 4)), dev(y=rem(y + 3, 4))
    z4 = dev(z=rem(z + 4, 8))
    up, down = dev(z=rem(z + 1, 8)), dev(z=rem(z + 7, 8))
    partner = dev(c=1 - c)
    has_up, has_down = zl < 3, zl > 0

    def remote(src, dst, send, recv, to):
        return pltpu.make_async_remote_copy(
            src_ref=src, dst_ref=dst, send_sem=send, recv_sem=recv,
            device_id=to, device_id_type=MESH,
        )

    krows = pl.ds(pl.multiple_of(c * K, K), K)
    w_local = pltpu.make_async_copy(w_hbm, w2.at[:, krows], loc.at[0])
    a_local = pltpu.make_async_copy(a_hbm, a2.at[0, krows, :], loc.at[1])
    f_local = pltpu.make_async_copy(fock_hbm, fock, loc.at[2])

    @pl.when(owner)
    def _():
        a_local.start()

    w_local.start()
    f_local.start()

    barrier = pltpu.get_barrier_semaphore()
    for to in (partner, xp, xm, yp, ym, z4):
        pl.semaphore_signal(barrier, inc=1, device_id=to, device_id_type=MESH)

    @pl.when(has_up)
    def _():
        pl.semaphore_signal(barrier, inc=1, device_id=up, device_id_type=MESH)

    @pl.when(has_down)
    def _():
        pl.semaphore_signal(barrier, inc=1, device_id=down, device_id_type=MESH)

    pl.semaphore_wait(barrier, 6 + has_up.astype(jnp.int32) + has_down.astype(jnp.int32))

    a_swap = remote(a_hbm, a2.at[0, krows, :], ax.at[0], ax.at[1], partner)
    w_swap = remote(w_hbm, w2.at[:, krows], wx.at[0], wx.at[1], partner)

    @pl.when(jnp.logical_not(owner))
    def _():
        a_swap.start()

    w_swap.start()

    def a_unit(ev, j):
        return a2.at[ev, :, pl.ds(j * HB, HB)]

    def a_wait(ev, j):
        remote(a_unit(ev, j), a_unit(ev, j), send_x.at[0, 0], recv_a.at[ev, j], xp).wait_recv()

    def a_send_x(direction, index, src, ev, j):
        return remote(
            src, a_unit(ev, j), send_x.at[direction, index], recv_a.at[ev, j],
            xp if direction == 0 else xm,
        )

    def a_sends_of(blk):
        ev = OWN[blk]
        s = f if blk == 0 else g
        origin = 2 * s + c
        zs, xs = [], []
        for h in range(2):
            there = div(zl + 1, 2)
            ev_up = jnp.where(s == there, OWN[0], OWN[1])
            zs.append((
                jnp.logical_and(has_up, zl >= origin),
                remote(a_unit(ev, h), a_unit(ev_up, h), send_z.at[blk, 0, h], recv_a.at[ev_up, h], up),
            ))
            below = div(zl + 1, 2) - 1
            ev_down = jnp.where(s == below, OWN[0], OWN[1])
            zs.append((
                jnp.logical_and(has_down, zl <= origin),
                remote(a_unit(ev, h), a_unit(ev_down, h), send_z.at[blk, 1, h], recv_a.at[ev_down, h], down),
            ))
        near, far = NEAR[blk], FAR[blk]
        for direction in range(2):
            for h in range(2):
                order = h if direction == 0 else 1 - h
                xs.append(a_send_x(
                    direction, 3 * blk + order, a_unit(ev, h), near if order == 0 else far, direction,
                ))
        return zs, xs

    def a_forwards(blk):
        return [a_send_x(d, 3 * blk + 2, a_unit(NEAR[blk], d), OPPOSITE[blk], d) for d in range(2)]

    def get_a(ev):
        if ev in OWN:
            zs, xs = a_sends_of(OWN.index(ev))
            if ev == 0:
                @pl.when(owner)
                def _():
                    a_local.wait()
                    remote(a_hbm, a2.at[0, pl.ds(pl.multiple_of((1 - c) * K, K), K), :], ax.at[0], ax.at[1], partner).wait_recv()
            for h in range(2):
                if ev == 0:
                    @pl.when(jnp.logical_not(owner))
                    def _():
                        a_wait(0, h)
                else:
                    a_wait(ev, h)
                for cond, copy in zs[2 * h:2 * h + 2]:
                    @pl.when(cond)
                    def _():
                        copy.start()
                if ev == 0:
                    xs[h].start()
            if ev == 0:
                xs[3].start()
                xs[2].start()
            else:
                forwards = a_forwards(0)
                xs[0].start()
                xs[3].start()
                forwards[0].start()
                forwards[1].start()
                xs[1].start()
                xs[2].start()
            return
        for j in range(2):
            a_wait(ev, j)
        if ev == NEAR[1]:
            for copy in a_forwards(1):
                copy.start()

    def compute(ev):
        def rows(i, _):
            at = pl.ds(pl.multiple_of(i * HM, HM), HM)
            cb[ev, at, :] = jnp.dot(w2[at, :], a2[ev], preferred_element_type=F32)
            return 0

        lax.fori_loop(0, 2, rows, 0)

    def chunk(i, second):
        return pl.ds(pl.multiple_of(i * CHUNK + second * (HM // 2), CHUNK), CHUNK)

    def packed(ref, values, i):
        numbers = []
        for k in range(2):
            high = values[k].astype(BF16)
            near = high.astype(F32)
            ref[chunk(i, k), :] = high
            size = jnp.maximum(jnp.abs(near), TINY)
            numbers.append(jnp.round((values[k] - near) * (pl.reciprocal(size, approx=True) * (1.0 / REST))))
        ref[chunk(i, 2), :] = (numbers[0] * BASE + numbers[1]).astype(BF16)

    def unpacked(ref, i):
        both = ref[chunk(i, 2), :].astype(F32)
        top = jnp.round(both * (1.0 / BASE))
        numbers = (top, both - top * BASE)
        values = []
        for k in range(2):
            high = ref[chunk(i, k), :].astype(F32)
            values.append(high + numbers[k] * (jnp.abs(high) * REST))
        return values

    def c_rows(ev, j, part, i, k):
        at = pl.ds(pl.multiple_of(part * HM + i * CHUNK + k * (HM // 2), CHUNK), CHUNK)
        return cb[ev, at, pl.ds(j * HB, HB)]

    def c_sum(ev, j, part, arrived, store):
        def step(i, _):
            values = [c_rows(ev, j, part, i, k) for k in range(2)]
            for ref in arrived:
                values = [a + b for a, b in zip(values, unpacked(ref, i))]
            store(i, values)
            return 0

        lax.fori_loop(0, HM // 2 // CHUNK, step, 0)

    def c_pack(ev, j, part, *arrived):
        c_sum(ev, j, part, arrived, lambda i, values: packed(sent.at[ev, j, part], values, i))

    def c_send(ev, j, part, dst, recv, to):
        return remote(sent.at[ev, j, part], dst, send_y.at[ev, j, part], recv, to)

    def place(ev, j):
        rel, far, h = UNITS[ev][j]
        xb = rem(x + (rel + 4), 4)
        s = g if far else f
        zd = div(xb, 2)
        yd = 2 * rem(xb, 2) + s
        return zd, rem(yd - y + 4, 4), h

    def to_half(ev, j, part, zd, h):
        slot = zd * 4 + part * 2 + h
        return c_send(ev, j, part, half.at[slot], r_half.at[slot], yp if part == 0 else ym)

    def to_full(ev, j, part, zd, h, side):
        slot = zd * 4 + side * 2 + h
        return c_send(
            ev, j, part, full.at[slot, part], r_full.at[slot, part],
            yp if side == 0 else ym,
        )

    def y_first(ev):
        for j in range(2):
            zd, r, h = place(ev, j)
            for part in range(2):
                @pl.when(jnp.logical_or(r == 2, r == 3 - 2 * part))
                def _():
                    c_pack(ev, j, part)

                @pl.when(r == 2)
                def _():
                    to_half(ev, j, part, zd, h).start()

                @pl.when(r == 3 - 2 * part)
                def _():
                    to_full(ev, j, part, zd, h, 1 - part).start()

    def y_second(ev):
        for j in range(2):
            zd, r, h = place(ev, j)
            for part in range(2):
                @pl.when(r == 1 + 2 * part)
                def _():
                    to_half(ev, j, part, zd, h).wait_recv()
                    c_pack(ev, j, part, half.at[zd * 4 + part * 2 + h])
                    to_full(ev, j, part, zd, h, part).start()

    def to_other(ev, j, part, h):
        return remote(
            sent.at[ev, j, part], rz.at[h, part], send_f.at[h, part], r_final.at[h, part], z4
        )

    def y_last(ev):
        for j in range(2):
            zd, r, h = place(ev, j)
            for part in range(2):
                arrived = [full.at[zd * 4 + side * 2 + h, part] for side in range(2)]

                @pl.when(r == 0)
                def _():
                    for side in range(2):
                        to_full(ev, j, part, zd, h, side).wait_recv()

                def keep(i, values):
                    for k in range(2):
                        racc[r_rows(part, i, k), pl.ds(h * HB, HB)] = values[k]

                @pl.when(jnp.logical_and(r == 0, zd == zh))
                def _():
                    c_sum(ev, j, part, arrived, keep)

                @pl.when(jnp.logical_and(r == 0, zd != zh))
                def _():
                    c_pack(ev, j, part, *arrived)
                    to_other(ev, j, part, h).start()

    def r_rows(part, i, k):
        return pl.ds(pl.multiple_of(part * HM + i * CHUNK + k * (HM // 2), CHUNK), CHUNK)

    def prepare():
        f_local.wait()
        fhi[...], flo[...] = split(fock[...])
        levels = jnp.broadcast_to(ev_ref[...], (128, V)).T
        here = ev_ref[:, pl.ds(pl.multiple_of(c * NB, NB), NB)]
        for i in range(M // V):
            pair = ei_ref[ia * (M // V) + i] + ej_ref[div(jb, 2)]
            for k in range(NB // 128):
                cols = pl.ds(k * 128, 128)
                denom = pair - levels - here[:, k * 128:(k + 1) * 128]
                rec[pl.ds(i * V, V), cols] = 1.0 / denom

    L2 = 1
    L3 = 3
    for step in range(EVENTS + L3):
        if step < EVENTS:
            get_a(step)
            if step == 0:
                w_local.wait()
                remote(w_hbm, w2.at[:, pl.ds(pl.multiple_of((1 - c) * K, K), K)], wx.at[0], wx.at[1], partner).wait_recv()
            compute(step)
            y_first(step)
            if step == 0:
                prepare()
        if 0 <= step - L2 < EVENTS:
            y_second(step - L2)
        if 0 <= step - L3 < EVENTS:
            y_last(step - L3)

    for h in range(2):
        for part in range(2):
            to_other(0, 0, part, h).wait_recv()

            def finish(i, _):
                values = unpacked(rz.at[h, part], i)
                for k in range(2):
                    at = (r_rows(part, i, k), pl.ds(h * HB, HB))
                    racc[at] = racc[at] + values[k]
                return 0

            lax.fori_loop(0, HM // 2 // CHUNK, finish, 0)

    swap = remote(racc, roth, cx.at[0], cx.at[1], partner)
    swap.start()

    mine = pl.ds(pl.multiple_of(c * NB, NB), NB)
    other = pl.ds(pl.multiple_of((1 - c) * NB, NB), NB)
    nn, nt = ((1,), (0,)), ((1,), (1,))
    for i in range(M // V):
        at = pl.ds(i * V, V)
        value = racc[at, :]
        parts = split(value)
        rows = value + dot3((fhi[...], flo[...]), parts, nn)
        out_ref[at, :] = rows + dot3(parts, (fhi[mine, mine], flo[mine, mine]), nt)
    swap.wait_recv()
    for i in range(M // V):
        at = pl.ds(i * V, V)
        parts = split(roth[at, :])
        out_ref[at, :] = (
            out_ref[at, :] + dot3(parts, (fhi[mine, other], flo[mine, other]), nt)
        ) * rec[at, :]

    swap.wait_send()
    w_swap.wait_send()

    @pl.when(jnp.logical_not(owner))
    def _():
        a_swap.wait_send()

    for blk in range(2):
        zs, xs = a_sends_of(blk)
        for cond, copy in zs:
            @pl.when(cond)
            def _():
                copy.wait_send()
        for copy in xs + a_forwards(blk):
            copy.wait_send()
    for ev in range(EVENTS):
        for j in range(2):
            zd, r, h = place(ev, j)

            @pl.when(r != 0)
            def _():
                for part in range(2):
                    to_half(ev, j, part, zd, h).wait_send()
    for h in range(2):
        for part in range(2):
            to_other(0, 0, part, h).wait_send()


def per_device(cycle_w, amplitudes, fock_vir, energy_i, energy_j, energy_vir):
    M, K = cycle_w.shape
    NB = amplitudes.shape[1]
    HB, HM = NB // 2, M // 2
    V = fock_vir.shape[0]
    dma = pltpu.SemaphoreType.DMA
    anywhere = pl.BlockSpec(memory_space=pl.ANY)
    vmem = pl.BlockSpec(memory_space=pltpu.VMEM)
    smem = pl.BlockSpec(memory_space=pltpu.SMEM)
    return pl.pallas_call(
        kernel,
        out_shape=jax.ShapeDtypeStruct((M, NB), F32),
        in_specs=[anywhere, anywhere, anywhere, smem, smem, vmem],
        out_specs=vmem,
        scratch_shapes=[
            pltpu.VMEM((M, 2 * K), BF16),
            pltpu.VMEM((EVENTS, 2 * K, NB), BF16),
            pltpu.VMEM((EVENTS, M, NB), F32),
            pltpu.VMEM((EVENTS, 2, 2, HM * 3 // 2, HB), BF16),
            pltpu.VMEM((8, 2, HM * 3 // 2, HB), BF16),
            pltpu.VMEM((8, HM * 3 // 2, HB), BF16),
            pltpu.VMEM((2, 2, HM * 3 // 2, HB), BF16),
            pltpu.VMEM((M, NB), F32),
            pltpu.VMEM((M, NB), F32),
            pltpu.VMEM((M, NB), F32),
            pltpu.VMEM((V, V), F32),
            pltpu.VMEM((V, V), BF16),
            pltpu.VMEM((V, V), BF16),
            dma((3,)), dma((2,)), dma((2,)), dma((EVENTS, 2)), dma((2, 6)), dma((2, 2, 2)),
            dma((8,)), dma((8, 2)), dma((EVENTS, 2, 2)),
            dma((2, 2)), dma((2, 2)), dma((2,)),
        ],
        compiler_params=pltpu.CompilerParams(
            collective_id=0, has_side_effects=True, vmem_limit_bytes=60 * 1024 * 1024
        ),
        name="residual",
    )(cycle_w, amplitudes, fock_vir, energy_i, energy_j, energy_vir.reshape(1, -1))


def solution(mesh):
    in_specs = (P("ia", "jb"), P("jb", "ia"), P(), P(), P(), P())
    out_specs = P("ia", "jb")
    return jax.shard_map(
        per_device, mesh=mesh, in_specs=in_specs, out_specs=out_specs, check_vma=False
    )
```

```python
import functools

import jax
import jax.numpy as jnp
from jax import lax
from jax.experimental import pallas as pl
from jax.experimental.pallas import tpu as pltpu
from jax.sharding import PartitionSpec as P

F32 = jnp.float32
BF16 = jnp.bfloat16
MESH = pl.DeviceIdType.MESH

UNITS = (
    ((0, 0, 0), (0, 0, 1)),
    ((-1, 0, 0), (1, 0, 1)),
    ((-1, 0, 1), (1, 0, 0)),
    ((0, 1, 0), (0, 1, 1)),
    ((2, 0, 0), (2, 0, 1)),
    ((-1, 1, 0), (1, 1, 1)),
    ((-1, 1, 1), (1, 1, 0)),
    ((2, 1, 0), (2, 1, 1)),
)
OWN, NEAR, FAR, OPPOSITE = (0, 3), (1, 5), (2, 6), (4, 7)
L2, L3 = 1, 3
EVENTS = len(UNITS)

LEVEL = 10
BASE = 2 * LEVEL + 1
REST = 2.0 ** -8 / LEVEL
TINY = 1e-30
CHUNK = 64


def div(a, b):
    return lax.div(a, jnp.int32(b))


def rem(a, b):
    return lax.rem(a, jnp.int32(b))


def split(value):
    high = value.astype(BF16)
    return high, (value - high.astype(F32)).astype(BF16)


def dot3(a, b, dims):
    dot = functools.partial(
        lax.dot_general, dimension_numbers=(dims, ((), ())), preferred_element_type=F32
    )
    return dot(a[0], b[0]) + (dot(a[0], b[1]) + dot(a[1], b[0]))


def kernel(
    w_hbm, a_hbm, fock_hbm, ei_ref, ej_ref, ev_ref, out_ref,
    w2, a2, cb, sent, full, half, rz, racc, roth, rec, fock, fhi, flo,
    loc, wx, ax, recv_a, send_x, send_z, r_half, r_full, send_y,
    send_f, r_final, cx,
):
    M, K = w_hbm.shape
    NB = a_hbm.shape[1]
    HB = NB // 2
    V = fock_hbm.shape[0]
    HM = M // 2

    ia = lax.axis_index("ia")
    jb = lax.axis_index("jb")
    x, zl = div(ia, 4), rem(ia, 4)
    zh, y, c = div(jb, 8), rem(div(jb, 2), 4), rem(jb, 2)
    z = zh * 4 + zl
    f = div(zl, 2)
    g = 1 - f
    owner = c == rem(zl, 2)

    def dev(x=x, y=y, z=z, c=c):
        return {"ia": x * 4 + rem(z, 4), "jb": div(z, 4) * 8 + y * 2 + c}

    xp, xm = dev(x=rem(x + 1, 4)), dev(x=rem(x + 3, 4))
    yp, ym = dev(y=rem(y + 1, 4)), dev(y=rem(y + 3, 4))
    z4 = dev(z=rem(z + 4, 8))
    up, down = dev(z=rem(z + 1, 8)), dev(z=rem(z + 7, 8))
    partner = dev(c=1 - c)
    has_up, has_down = zl < 3, zl > 0

    def remote(src, dst, send, recv, to):
        return pltpu.make_async_remote_copy(
            src_ref=src, dst_ref=dst, send_sem=send, recv_sem=recv,
            device_id=to, device_id_type=MESH,
        )

    krows = pl.ds(pl.multiple_of(c * K, K), K)
    w_local = pltpu.make_async_copy(w_hbm, w2.at[:, krows], loc.at[0])
    a_local = pltpu.make_async_copy(a_hbm, a2.at[0, krows, :], loc.at[1])
    f_local = pltpu.make_async_copy(fock_hbm, fock, loc.at[2])

    @pl.when(owner)
    def _():
        a_local.start()

    w_local.start()
    f_local.start()

    barrier = pltpu.get_barrier_semaphore()
    for to in (partner, xp, xm, yp, ym, z4):
        pl.semaphore_signal(barrier, inc=1, device_id=to, device_id_type=MESH)

    @pl.when(has_up)
    def _():
        pl.semaphore_signal(barrier, inc=1, device_id=up, device_id_type=MESH)

    @pl.when(has_down)
    def _():
        pl.semaphore_signal(barrier, inc=1, device_id=down, device_id_type=MESH)

    pl.semaphore_wait(barrier, 6 + has_up.astype(jnp.int32) + has_down.astype(jnp.int32))

    a_swap = remote(a_hbm, a2.at[0, krows, :], ax.at[0], ax.at[1], partner)
    w_swap = remote(w_hbm, w2.at[:, krows], wx.at[0], wx.at[1], partner)

    @pl.when(jnp.logical_not(owner))
    def _():
        a_swap.start()

    w_swap.start()

    def a_unit(ev, j):
        return a2.at[ev, :, pl.ds(j * HB, HB)]

    def a_wait(ev, j):
        remote(a_unit(ev, j), a_unit(ev, j), send_x.at[0, 0], recv_a.at[ev, j], xp).wait_recv()

    def a_send_x(direction, index, src, ev, j):
        return remote(
            src, a_unit(ev, j), send_x.at[direction, index], recv_a.at[ev, j],
            xp if direction == 0 else xm,
        )

    def a_sends_of(blk):
        ev = OWN[blk]
        s = f if blk == 0 else g
        origin = 2 * s + c
        zs, xs = [], []
        for h in range(2):
            there = div(zl + 1, 2)
            ev_up = jnp.where(s == there, OWN[0], OWN[1])
            zs.append((
                jnp.logical_and(has_up, zl >= origin),
                remote(a_unit(ev, h), a_unit(ev_up, h), send_z.at[blk, 0, h], recv_a.at[ev_up, h], up),
            ))
            below = div(zl + 1, 2) - 1
            ev_down = jnp.where(s == below, OWN[0], OWN[1])
            zs.append((
                jnp.logical_and(has_down, zl <= origin),
                remote(a_unit(ev, h), a_unit(ev_down, h), send_z.at[blk, 1, h], recv_a.at[ev_down, h], down),
            ))
        near, far = NEAR[blk], FAR[blk]
        for direction in range(2):
            for h in range(2):
                order = h if direction == 0 else 1 - h
                xs.append(a_send_x(
                    direction, 3 * blk + order, a_unit(ev, h), near if order == 0 else far, direction,
                ))
        return zs, xs

    def a_forwards(blk):
        return [a_send_x(d, 3 * blk + 2, a_unit(NEAR[blk], d), OPPOSITE[blk], d) for d in range(2)]

    def get_a(ev):
        if ev in OWN:
            blk = OWN.index(ev)
            zs, xs = a_sends_of(blk)
            if blk == 0:
                @pl.when(owner)
                def _():
                    a_local.wait()
                    remote(a_hbm, a2.at[0, pl.ds(pl.multiple_of((1 - c) * K, K), K), :], ax.at[0], ax.at[1], partner).wait_recv()
            for h in range(2):
                if blk == 0:
                    @pl.when(jnp.logical_not(owner))
                    def _():
                        a_wait(0, h)
                else:
                    a_wait(ev, h)
                for cond, copy in zs[2 * h:2 * h + 2]:
                    @pl.when(cond)
                    def _():
                        copy.start()
                xs[h].start()
            xs[3].start()
            xs[2].start()
            return
        for j in range(2):
            a_wait(ev, j)
            if ev in NEAR:
                a_forwards(NEAR.index(ev))[j].start()

    def compute(ev):
        def rows(i, _):
            at = pl.ds(pl.multiple_of(i * HM, HM), HM)
            cb[ev, at, :] = jnp.dot(w2[at, :], a2[ev], preferred_element_type=F32)
            return 0

        lax.fori_loop(0, 2, rows, 0)

    def chunk(i, second):
        return pl.ds(pl.multiple_of(i * CHUNK + second * (HM // 2), CHUNK), CHUNK)

    def packed(ref, values, i):
        numbers = []
        for k in range(2):
            high = values[k].astype(BF16)
            near = high.astype(F32)
            ref[chunk(i, k), :] = high
            size = jnp.maximum(jnp.abs(near), TINY)
            numbers.append(jnp.round((values[k] - near) * (pl.reciprocal(size, approx=True) * (1.0 / REST))))
        ref[chunk(i, 2), :] = (numbers[0] * BASE + numbers[1]).astype(BF16)

    def unpacked(ref, i):
        both = ref[chunk(i, 2), :].astype(F32)
        top = jnp.round(both * (1.0 / BASE))
        numbers = (top, both - top * BASE)
        values = []
        for k in range(2):
            high = ref[chunk(i, k), :].astype(F32)
            values.append(high + numbers[k] * (jnp.abs(high) * REST))
        return values

    def c_rows(ev, j, part, i, k):
        at = pl.ds(pl.multiple_of(part * HM + i * CHUNK + k * (HM // 2), CHUNK), CHUNK)
        return cb[ev, at, pl.ds(j * HB, HB)]

    def c_sum(ev, j, part, arrived, store):
        def step(i, _):
            values = [c_rows(ev, j, part, i, k) for k in range(2)]
            for ref in arrived:
                values = [a + b for a, b in zip(values, unpacked(ref, i))]
            store(i, values)
            return 0

        lax.fori_loop(0, HM // 2 // CHUNK, step, 0)

    def c_pack(ev, j, part, *arrived):
        c_sum(ev, j, part, arrived, lambda i, values: packed(sent.at[ev, j, part], values, i))

    def c_send(ev, j, part, dst, recv, to):
        return remote(sent.at[ev, j, part], dst, send_y.at[ev, j, part], recv, to)

    def place(ev, j):
        rel, far, h = UNITS[ev][j]
        xb = rem(x + (rel + 4), 4)
        s = g if far else f
        zd = div(xb, 2)
        yd = 2 * rem(xb, 2) + s
        return zd, rem(yd - y + 4, 4), h

    def to_half(ev, j, part, zd, h):
        slot = zd * 4 + part * 2 + h
        return c_send(ev, j, part, half.at[slot], r_half.at[slot], yp if part == 0 else ym)

    def to_full(ev, j, part, zd, h, side):
        slot = zd * 4 + side * 2 + h
        return c_send(
            ev, j, part, full.at[slot, part], r_full.at[slot, part],
            yp if side == 0 else ym,
        )

    def y_first(ev):
        for j in range(2):
            zd, r, h = place(ev, j)
            for part in range(2):
                @pl.when(jnp.logical_or(r == 2, r == 3 - 2 * part))
                def _():
                    c_pack(ev, j, part)

                @pl.when(r == 2)
                def _():
                    to_half(ev, j, part, zd, h).start()

                @pl.when(r == 3 - 2 * part)
                def _():
                    to_full(ev, j, part, zd, h, 1 - part).start()

    def y_second(ev):
        for j in range(2):
            zd, r, h = place(ev, j)
            for part in range(2):
                @pl.when(r == 1 + 2 * part)
                def _():
                    to_half(ev, j, part, zd, h).wait_recv()
                    c_pack(ev, j, part, half.at[zd * 4 + part * 2 + h])
                    to_full(ev, j, part, zd, h, part).start()

    def to_other(ev, j, part, h):
        return remote(
            sent.at[ev, j, part], rz.at[h, part], send_f.at[h, part], r_final.at[h, part], z4
        )

    def y_last(ev):
        for j in range(2):
            zd, r, h = place(ev, j)
            for part in range(2):
                arrived = [full.at[zd * 4 + side * 2 + h, part] for side in range(2)]

                @pl.when(r == 0)
                def _():
                    for side in range(2):
                        to_full(ev, j, part, zd, h, side).wait_recv()

                def keep(i, values):
                    for k in range(2):
                        racc[r_rows(part, i, k), pl.ds(h * HB, HB)] = values[k]

                @pl.when(jnp.logical_and(r == 0, zd == zh))
                def _():
                    c_sum(ev, j, part, arrived, keep)

                @pl.when(jnp.logical_and(r == 0, zd != zh))
                def _():
                    c_pack(ev, j, part, *arrived)
                    to_other(ev, j, part, h).start()

    def r_rows(part, i, k):
        return pl.ds(pl.multiple_of(part * HM + i * CHUNK + k * (HM // 2), CHUNK), CHUNK)

    def prepare():
        f_local.wait()
        fhi[...], flo[...] = split(fock[...])
        levels = jnp.broadcast_to(ev_ref[...], (128, V)).T
        here = ev_ref[:, pl.ds(pl.multiple_of(c * NB, NB), NB)]
        for i in range(M // V):
            pair = ei_ref[ia * (M // V) + i] + ej_ref[div(jb, 2)]
            for k in range(NB // 128):
                cols = pl.ds(k * 128, 128)
                denom = pair - levels - here[:, k * 128:(k + 1) * 128]
                rec[pl.ds(i * V, V), cols] = 1.0 / denom

    for step in range(EVENTS + L3):
        if step < EVENTS:
            get_a(step)
            if step == 0:
                w_local.wait()
                remote(w_hbm, w2.at[:, pl.ds(pl.multiple_of((1 - c) * K, K), K)], wx.at[0], wx.at[1], partner).wait_recv()
            compute(step)
            y_first(step)
            if step == 0:
                prepare()
        if 0 <= step - L2 < EVENTS:
            y_second(step - L2)
        if 0 <= step - L3 < EVENTS:
            y_last(step - L3)

    for h in range(2):
        for part in range(2):
            to_other(0, 0, part, h).wait_recv()

            def finish(i, _):
                values = unpacked(rz.at[h, part], i)
                for k in range(2):
                    at = (r_rows(part, i, k), pl.ds(h * HB, HB))
                    racc[at] = racc[at] + values[k]
                return 0

            lax.fori_loop(0, HM // 2 // CHUNK, finish, 0)

    swap = remote(racc, roth, cx.at[0], cx.at[1], partner)
    swap.start()

    mine = pl.ds(pl.multiple_of(c * NB, NB), NB)
    other = pl.ds(pl.multiple_of((1 - c) * NB, NB), NB)
    nn, nt = ((1,), (0,)), ((1,), (1,))
    for i in range(M // V):
        at = pl.ds(i * V, V)
        value = racc[at, :]
        parts = split(value)
        rows = value + dot3((fhi[...], flo[...]), parts, nn)
        out_ref[at, :] = rows + dot3(parts, (fhi[mine, mine], flo[mine, mine]), nt)
    swap.wait_recv()
    for i in range(M // V):
        at = pl.ds(i * V, V)
        parts = split(roth[at, :])
        out_ref[at, :] = (
            out_ref[at, :] + dot3(parts, (fhi[mine, other], flo[mine, other]), nt)
        ) * rec[at, :]

    swap.wait_send()
    w_swap.wait_send()

    @pl.when(jnp.logical_not(owner))
    def _():
        a_swap.wait_send()

    for blk in range(2):
        zs, xs = a_sends_of(blk)
        for cond, copy in zs:
            @pl.when(cond)
            def _():
                copy.wait_send()
        for copy in xs + a_forwards(blk):
            copy.wait_send()
    for ev in range(EVENTS):
        for j in range(2):
            zd, r, h = place(ev, j)

            @pl.when(r != 0)
            def _():
                for part in range(2):
                    to_half(ev, j, part, zd, h).wait_send()
    for h in range(2):
        for part in range(2):
            to_other(0, 0, part, h).wait_send()


def per_device(cycle_w, amplitudes, fock_vir, energy_i, energy_j, energy_vir):
    M, K = cycle_w.shape
    NB = amplitudes.shape[1]
    HB, HM = NB // 2, M // 2
    V = fock_vir.shape[0]
    dma = pltpu.SemaphoreType.DMA
    anywhere = pl.BlockSpec(memory_space=pl.ANY)
    vmem = pl.BlockSpec(memory_space=pltpu.VMEM)
    smem = pl.BlockSpec(memory_space=pltpu.SMEM)
    return pl.pallas_call(
        kernel,
        out_shape=jax.ShapeDtypeStruct((M, NB), F32),
        in_specs=[anywhere, anywhere, anywhere, smem, smem, vmem],
        out_specs=vmem,
        scratch_shapes=[
            pltpu.VMEM((M, 2 * K), BF16),
            pltpu.VMEM((EVENTS, 2 * K, NB), BF16),
            pltpu.VMEM((EVENTS, M, NB), F32),
            pltpu.VMEM((EVENTS, 2, 2, HM * 3 // 2, HB), BF16),
            pltpu.VMEM((8, 2, HM * 3 // 2, HB), BF16),
            pltpu.VMEM((8, HM * 3 // 2, HB), BF16),
            pltpu.VMEM((2, 2, HM * 3 // 2, HB), BF16),
            pltpu.VMEM((M, NB), F32),
            pltpu.VMEM((M, NB), F32),
            pltpu.VMEM((M, NB), F32),
            pltpu.VMEM((V, V), F32),
            pltpu.VMEM((V, V), BF16),
            pltpu.VMEM((V, V), BF16),
            dma((3,)), dma((2,)), dma((2,)), dma((EVENTS, 2)), dma((2, 6)), dma((2, 2, 2)),
            dma((8,)), dma((8, 2)), dma((EVENTS, 2, 2)),
            dma((2, 2)), dma((2, 2)), dma((2,)),
        ],
        compiler_params=pltpu.CompilerParams(
            collective_id=0, has_side_effects=True, vmem_limit_bytes=60 * 1024 * 1024
        ),
        name="residual",
    )(cycle_w, amplitudes, fock_vir, energy_i, energy_j, energy_vir.reshape(1, -1))


def solution(mesh):
    in_specs = (P("ia", "jb"), P("jb", "ia"), P(), P(), P(), P())
    out_specs = P("ia", "jb")
    return jax.shard_map(
        per_device, mesh=mesh, in_specs=in_specs, out_specs=out_specs, check_vma=False
    )
```

```python
import functools

import jax
import jax.numpy as jnp
from jax import lax
from jax.experimental import pallas as pl
from jax.experimental.pallas import tpu as pltpu
from jax.sharding import PartitionSpec as P

F32 = jnp.float32
BF16 = jnp.bfloat16
MESH = pl.DeviceIdType.MESH

UNITS = (
    ((0, 0, 0), (0, 0, 1)),
    ((-1, 0, 0), (1, 0, 1)),
    ((-1, 0, 1), (1, 0, 0)),
    ((0, 1, 0), (0, 1, 1)),
    ((2, 0, 0), (2, 0, 1)),
    ((-1, 1, 0), (1, 1, 1)),
    ((-1, 1, 1), (1, 1, 0)),
    ((2, 1, 0), (2, 1, 1)),
)
OWN, NEAR, FAR, OPPOSITE = (0, 3), (1, 5), (2, 6), (4, 7)
L2, L3 = 1, 3
EVENTS = len(UNITS)

LEVEL = 10
BASE = 2 * LEVEL + 1
REST = 2.0 ** -8 / LEVEL
TINY = 1e-30
CHUNK = 64


def div(a, b):
    return lax.div(a, jnp.int32(b))


def rem(a, b):
    return lax.rem(a, jnp.int32(b))


def split(value):
    high = value.astype(BF16)
    return high, (value - high.astype(F32)).astype(BF16)


def dot3(a, b, dims):
    dot = functools.partial(
        lax.dot_general, dimension_numbers=(dims, ((), ())), preferred_element_type=F32
    )
    return dot(a[0], b[0]) + (dot(a[0], b[1]) + dot(a[1], b[0]))


def kernel(
    w_hbm, a_hbm, fock_hbm, ei_ref, ej_ref, ev_ref, out_ref,
    w2, a2, cb, sent, full, half, rz, racc, roth, rec, fock, fhi, flo,
    loc, wx, ax, recv_a, send_x, send_z, r_half, r_full, send_y,
    send_f, r_final, cx,
):
    M, K = w_hbm.shape
    NB = a_hbm.shape[1]
    HB = NB // 2
    V = fock_hbm.shape[0]
    HM = M // 2

    ia = lax.axis_index("ia")
    jb = lax.axis_index("jb")
    x, zl = div(ia, 4), rem(ia, 4)
    zh, y, c = div(jb, 8), rem(div(jb, 2), 4), rem(jb, 2)
    z = zh * 4 + zl
    f = div(zl, 2)
    g = 1 - f
    owner = c == rem(zl, 2)

    def dev(x=x, y=y, z=z, c=c):
        return {"ia": x * 4 + rem(z, 4), "jb": div(z, 4) * 8 + y * 2 + c}

    xp, xm = dev(x=rem(x + 1, 4)), dev(x=rem(x + 3, 4))
    yp, ym = dev(y=rem(y + 1, 4)), dev(y=rem(y + 3, 4))
    z4 = dev(z=rem(z + 4, 8))
    up, down = dev(z=rem(z + 1, 8)), dev(z=rem(z + 7, 8))
    partner = dev(c=1 - c)
    has_up, has_down = zl < 3, zl > 0

    def remote(src, dst, send, recv, to):
        return pltpu.make_async_remote_copy(
            src_ref=src, dst_ref=dst, send_sem=send, recv_sem=recv,
            device_id=to, device_id_type=MESH,
        )

    krows = pl.ds(pl.multiple_of(c * K, K), K)
    w_local = pltpu.make_async_copy(w_hbm, w2.at[:, krows], loc.at[0])
    a_local = pltpu.make_async_copy(a_hbm, a2.at[0, krows, :], loc.at[1])
    f_local = pltpu.make_async_copy(fock_hbm, fock, loc.at[2])

    @pl.when(owner)
    def _():
        a_local.start()

    w_local.start()
    f_local.start()

    barrier = pltpu.get_barrier_semaphore()
    for to in (partner, xp, xm, yp, ym, z4):
        pl.semaphore_signal(barrier, inc=1, device_id=to, device_id_type=MESH)

    @pl.when(has_up)
    def _():
        pl.semaphore_signal(barrier, inc=1, device_id=up, device_id_type=MESH)

    @pl.when(has_down)
    def _():
        pl.semaphore_signal(barrier, inc=1, device_id=down, device_id_type=MESH)

    pl.semaphore_wait(barrier, 6 + has_up.astype(jnp.int32) + has_down.astype(jnp.int32))

    a_swap = remote(a_hbm, a2.at[0, krows, :], ax.at[0], ax.at[1], partner)
    w_swap = remote(w_hbm, w2.at[:, krows], wx.at[0], wx.at[1], partner)

    @pl.when(jnp.logical_not(owner))
    def _():
        a_swap.start()

    w_swap.start()

    def a_unit(ev, j):
        return a2.at[ev, :, pl.ds(j * HB, HB)]

    def a_wait(ev, j):
        remote(a_unit(ev, j), a_unit(ev, j), send_x.at[0, 0], recv_a.at[ev, j], xp).wait_recv()

    def a_send_x(direction, index, src, ev, j):
        return remote(
            src, a_unit(ev, j), send_x.at[direction, index], recv_a.at[ev, j],
            xp if direction == 0 else xm,
        )

    def a_sends_of(blk):
        ev = OWN[blk]
        s = f if blk == 0 else g
        origin = 2 * s + c
        zs, xs = [], []
        for h in range(2):
            there = div(zl + 1, 2)
            ev_up = jnp.where(s == there, OWN[0], OWN[1])
            zs.append((
                jnp.logical_and(has_up, zl >= origin),
                remote(a_unit(ev, h), a_unit(ev_up, h), send_z.at[blk, 0, h], recv_a.at[ev_up, h], up),
            ))
            below = div(zl + 1, 2) - 1
            ev_down = jnp.where(s == below, OWN[0], OWN[1])
            zs.append((
                jnp.logical_and(has_down, zl <= origin),
                remote(a_unit(ev, h), a_unit(ev_down, h), send_z.at[blk, 1, h], recv_a.at[ev_down, h], down),
            ))
        near, far = NEAR[blk], FAR[blk]
        for direction in range(2):
            for h in range(2):
                order = h if direction == 0 else 1 - h
                xs.append(a_send_x(
                    direction, 3 * blk + order, a_unit(ev, h), near if order == 0 else far, direction,
                ))
        return zs, xs

    def a_forwards(blk):
        return [a_send_x(d, 3 * blk + 2, a_unit(NEAR[blk], d), OPPOSITE[blk], d) for d in range(2)]

    def get_a(ev):
        if ev in OWN:
            blk = OWN.index(ev)
            zs, xs = a_sends_of(blk)
            if blk == 0:
                @pl.when(owner)
                def _():
                    a_local.wait()
                    remote(a_hbm, a2.at[0, pl.ds(pl.multiple_of((1 - c) * K, K), K), :], ax.at[0], ax.at[1], partner).wait_recv()
            for h in range(2):
                if blk == 0:
                    @pl.when(jnp.logical_not(owner))
                    def _():
                        a_wait(0, h)
                else:
                    a_wait(ev, h)
                for cond, copy in zs[2 * h:2 * h + 2]:
                    @pl.when(cond)
                    def _():
                        copy.start()
                xs[h].start()
            xs[3].start()
            xs[2].start()
            return
        for j in range(2):
            a_wait(ev, j)
            if ev in NEAR:
                a_forwards(NEAR.index(ev))[j].start()

    def compute(ev):
        def rows(i, _):
            at = pl.ds(pl.multiple_of(i * HM, HM), HM)
            cb[ev, at, :] = jnp.dot(w2[at, :], a2[ev], preferred_element_type=F32)
            return 0

        lax.fori_loop(0, 2, rows, 0)

    def chunk(i, second):
        return pl.ds(pl.multiple_of(i * CHUNK + second * (HM // 2), CHUNK), CHUNK)

    def packed(ref, values, i):
        numbers = []
        for k in range(2):
            high = values[k].astype(BF16)
            near = high.astype(F32)
            ref[chunk(i, k), :] = high
            size = jnp.maximum(jnp.abs(near), TINY)
            numbers.append(jnp.round((values[k] - near) * (pl.reciprocal(size, approx=True) * (1.0 / REST))))
        ref[chunk(i, 2), :] = (numbers[0] * BASE + numbers[1]).astype(BF16)

    def unpacked(ref, i):
        both = ref[chunk(i, 2), :].astype(F32)
        top = jnp.round(both * (1.0 / BASE))
        numbers = (top, both - top * BASE)
        values = []
        for k in range(2):
            high = ref[chunk(i, k), :].astype(F32)
            values.append(high + numbers[k] * (jnp.abs(high) * REST))
        return values

    def c_rows(ev, j, part, i, k):
        at = pl.ds(pl.multiple_of(part * HM + i * CHUNK + k * (HM // 2), CHUNK), CHUNK)
        return cb[ev, at, pl.ds(j * HB, HB)]

    def c_sum(ev, j, part, arrived, store):
        def step(i, _):
            values = [c_rows(ev, j, part, i, k) for k in range(2)]
            for ref in arrived:
                values = [a + b for a, b in zip(values, unpacked(ref, i))]
            store(i, values)
            return 0

        lax.fori_loop(0, HM // 2 // CHUNK, step, 0)

    def c_pack(ev, j, part, *arrived):
        c_sum(ev, j, part, arrived, lambda i, values: packed(sent.at[ev, j, part], values, i))

    def c_send(ev, j, part, dst, recv, to):
        return remote(sent.at[ev, j, part], dst, send_y.at[ev, j, part], recv, to)

    def place(ev, j):
        rel, far, h = UNITS[ev][j]
        xb = rem(x + (rel + 4), 4)
        s = g if far else f
        zd = div(xb, 2)
        yd = 2 * rem(xb, 2) + s
        return zd, rem(yd - y + 4, 4), h

    def to_half(ev, j, part, zd, h):
        slot = zd * 4 + part * 2 + h
        return c_send(ev, j, part, half.at[slot], r_half.at[slot], yp if part == 0 else ym)

    def to_full(ev, j, part, zd, h, side):
        slot = zd * 4 + side * 2 + h
        return c_send(
            ev, j, part, full.at[slot, part], r_full.at[slot, part],
            yp if side == 0 else ym,
        )

    def y_first(ev):
        for j in range(2):
            zd, r, h = place(ev, j)
            for part in range(2):
                @pl.when(jnp.logical_or(r == 2, r == 3 - 2 * part))
                def _():
                    c_pack(ev, j, part)

                @pl.when(r == 2)
                def _():
                    to_half(ev, j, part, zd, h).start()

                @pl.when(r == 3 - 2 * part)
                def _():
                    to_full(ev, j, part, zd, h, 1 - part).start()

    def y_second(ev):
        for j in range(2):
            zd, r, h = place(ev, j)
            for part in range(2):
                @pl.when(r == 1 + 2 * part)
                def _():
                    to_half(ev, j, part, zd, h).wait_recv()
                    c_pack(ev, j, part, half.at[zd * 4 + part * 2 + h])
                    to_full(ev, j, part, zd, h, part).start()

    def to_other(ev, j, part, h):
        return remote(
            sent.at[ev, j, part], rz.at[h, part], send_f.at[h, part], r_final.at[h, part], z4
        )

    def y_last(ev):
        for j in range(2):
            zd, r, h = place(ev, j)
            for part in range(2):
                arrived = [full.at[zd * 4 + side * 2 + h, part] for side in range(2)]

                @pl.when(r == 0)
                def _():
                    for side in range(2):
                        to_full(ev, j, part, zd, h, side).wait_recv()

                def keep(i, values):
                    for k in range(2):
                        racc[r_rows(part, i, k), pl.ds(h * HB, HB)] = values[k]

                @pl.when(jnp.logical_and(r == 0, zd == zh))
                def _():
                    c_sum(ev, j, part, arrived, keep)

                @pl.when(jnp.logical_and(r == 0, zd != zh))
                def _():
                    c_pack(ev, j, part, *arrived)
                    to_other(ev, j, part, h).start()

    def r_rows(part, i, k):
        return pl.ds(pl.multiple_of(part * HM + i * CHUNK + k * (HM // 2), CHUNK), CHUNK)

    def prepare():
        f_local.wait()
        fhi[...], flo[...] = split(fock[...])
        levels = jnp.broadcast_to(ev_ref[...], (128, V)).T
        here = ev_ref[:, pl.ds(pl.multiple_of(c * NB, NB), NB)]
        for i in range(M // V):
            pair = ei_ref[ia * (M // V) + i] + ej_ref[div(jb, 2)]
            for k in range(NB // 128):
                cols = pl.ds(k * 128, 128)
                denom = pair - levels - here[:, k * 128:(k + 1) * 128]
                rec[pl.ds(i * V, V), cols] = 1.0 / denom

    for step in range(EVENTS + L3):
        if step < EVENTS:
            get_a(step)
            if step == 0:
                w_local.wait()
                remote(w_hbm, w2.at[:, pl.ds(pl.multiple_of((1 - c) * K, K), K)], wx.at[0], wx.at[1], partner).wait_recv()
            compute(step)
            y_first(step)
            if step == 0:
                prepare()
        if 0 <= step - L2 < EVENTS:
            y_second(step - L2)
        if 0 <= step - L3 < EVENTS:
            y_last(step - L3)

    mine = pl.ds(pl.multiple_of(c * NB, NB), NB)
    other = pl.ds(pl.multiple_of((1 - c) * NB, NB), NB)
    nn, nt = ((1,), (0,)), ((1,), (1,))

    def swap(part):
        at = pl.ds(part * HM, HM)
        return remote(racc.at[at, :], roth.at[at, :], cx.at[0, part], cx.at[1, part], partner)

    for part in range(2):
        for h in range(2):
            to_other(0, 0, part, h).wait_recv()

            def finish(i, _):
                values = unpacked(rz.at[h, part], i)
                for k in range(2):
                    at = (r_rows(part, i, k), pl.ds(h * HB, HB))
                    racc[at] = racc[at] + values[k]
                return 0

            lax.fori_loop(0, HM // 2 // CHUNK, finish, 0)
        swap(part).start()
        at = pl.ds(part * HM, HM)
        value = racc[at, :]
        parts = split(value)
        rows = value + dot3((fhi[...], flo[...]), parts, nn)
        out_ref[at, :] = rows + dot3(parts, (fhi[mine, mine], flo[mine, mine]), nt)
    for part in range(2):
        swap(part).wait_recv()
        at = pl.ds(part * HM, HM)
        parts = split(roth[at, :])
        out_ref[at, :] = (
            out_ref[at, :] + dot3(parts, (fhi[mine, other], flo[mine, other]), nt)
        ) * rec[at, :]

    for part in range(2):
        swap(part).wait_send()
    w_swap.wait_send()

    @pl.when(jnp.logical_not(owner))
    def _():
        a_swap.wait_send()

    for blk in range(2):
        zs, xs = a_sends_of(blk)
        for cond, copy in zs:
            @pl.when(cond)
            def _():
                copy.wait_send()
        for copy in xs + a_forwards(blk):
            copy.wait_send()
    for ev in range(EVENTS):
        for j in range(2):
            zd, r, h = place(ev, j)

            @pl.when(r != 0)
            def _():
                for part in range(2):
                    to_half(ev, j, part, zd, h).wait_send()
    for h in range(2):
        for part in range(2):
            to_other(0, 0, part, h).wait_send()


def per_device(cycle_w, amplitudes, fock_vir, energy_i, energy_j, energy_vir):
    M, K = cycle_w.shape
    NB = amplitudes.shape[1]
    HB, HM = NB // 2, M // 2
    V = fock_vir.shape[0]
    dma = pltpu.SemaphoreType.DMA
    anywhere = pl.BlockSpec(memory_space=pl.ANY)
    vmem = pl.BlockSpec(memory_space=pltpu.VMEM)
    smem = pl.BlockSpec(memory_space=pltpu.SMEM)
    return pl.pallas_call(
        kernel,
        out_shape=jax.ShapeDtypeStruct((M, NB), F32),
        in_specs=[anywhere, anywhere, anywhere, smem, smem, vmem],
        out_specs=vmem,
        scratch_shapes=[
            pltpu.VMEM((M, 2 * K), BF16),
            pltpu.VMEM((EVENTS, 2 * K, NB), BF16),
            pltpu.VMEM((EVENTS, M, NB), F32),
            pltpu.VMEM((EVENTS, 2, 2, HM * 3 // 2, HB), BF16),
            pltpu.VMEM((8, 2, HM * 3 // 2, HB), BF16),
            pltpu.VMEM((8, HM * 3 // 2, HB), BF16),
            pltpu.VMEM((2, 2, HM * 3 // 2, HB), BF16),
            pltpu.VMEM((M, NB), F32),
            pltpu.VMEM((M, NB), F32),
            pltpu.VMEM((M, NB), F32),
            pltpu.VMEM((V, V), F32),
            pltpu.VMEM((V, V), BF16),
            pltpu.VMEM((V, V), BF16),
            dma((3,)), dma((2,)), dma((2,)), dma((EVENTS, 2)), dma((2, 6)), dma((2, 2, 2)),
            dma((8,)), dma((8, 2)), dma((EVENTS, 2, 2)),
            dma((2, 2)), dma((2, 2)), dma((2, 2)),
        ],
        compiler_params=pltpu.CompilerParams(
            collective_id=0, has_side_effects=True, vmem_limit_bytes=60 * 1024 * 1024
        ),
        name="residual",
    )(cycle_w, amplitudes, fock_vir, energy_i, energy_j, energy_vir.reshape(1, -1))


def solution(mesh):
    in_specs = (P("ia", "jb"), P("jb", "ia"), P(), P(), P(), P())
    out_specs = P("ia", "jb")
    return jax.shard_map(
        per_device, mesh=mesh, in_specs=in_specs, out_specs=out_specs, check_vma=False
    )
```
